32 devices in a mesh: groups: 2 (over y), row: 2 (over x), col: 4 (over z), dp: 2 (over core).
Axes of the slice: x: 2, y: 2, z: 4, core: 2. Of those that a mesh axis runs over, the one named last changes fastest.
Arguments:
- features: bfloat16 [4, 512, 6144], P(('groups', 'dp'), 'row', 'col'), parts along dimension 0, may hold values from -6 to 6
- output_gradient: bfloat16 [4, 512, 6144], P(('groups', 'dp'), 'row', 'col'), parts along dimension 0, may hold values from -6 to 6
- value_weight: bfloat16 [6144, 6144], P('row', 'col'), may hold values from -0.109375 to 0.109375
- gate_weight: bfloat16 [6144, 6144], P('row', 'col'), may hold values from -1 to 1
- mixer_weight: bfloat16 [6144, 6144], P('row', 'col'), may hold values from -0.109375 to 0.109375
- conv_kernel: float32 [31, 6144], P(None, 'col'), may hold values from -1 to 1
- layer_norm_gain: float32 [6144], replicated, may hold values from 0.3 to 4.2
Outputs:
- module_out: bfloat16 [4, 512, 6144], P(('groups', 'dp'), 'row', 'col'), parts along dimension 0
- input_gradient: bfloat16 [4, 512, 6144], P(('groups', 'dp'), 'row', 'col'), parts along dimension 0
- value_weight_grad: float32 [12288, 6144], P(('groups', 'row', 'dp'), 'col'), parts along dimension 0
- gate_weight_grad: float32 [12288, 6144], P(('groups', 'row', 'dp'), 'col'), parts along dimension 0
- mixer_weight_grad: float32 [12288, 6144], P(('groups', 'row', 'dp'), 'col'), parts along dimension 0
- kernel_grad: float32 [62, 6144], P('groups', 'col'), parts along dimension 0
- norm_gain_gradient: float32 [12288], P(('groups', 'col')), parts along dimension 0
The draws below stay inside these ranges and needn't reach their ends.
There are 2 independent parts, one for each index of `groups`. The reference program is written for one: setup_inputs(seed, part) draws one part's arguments, and reference() takes and returns one part's arrays. A program takes and returns all parts, laid end to end along the dimension named above; an argument that names none is the same for every part. Nothing has to cross between parts.
All inputs are finite; a program needn't handle non-finite values.
Results may differ from the reference program's by a relative error of at most 0.02.
Values may be sent and summed in bfloat16 or wider, within the bound.
A program may use at most 320 MiB of HBM per device.

```python
import math
import jax
import jax.numpy as jnp
from jax import lax

MODEL_WIDTH = 6144
KERNEL = 31
TF_DEV = 256
UTT_DEV = 1
FRAMES = 512
UTT = 2
N_ROW = 2
N_COL = 4
N_DP = 2


def draw_layer_norm_gain(key, part):
    position = jnp.arange(MODEL_WIDTH, dtype=jnp.float32) / (MODEL_WIDTH - 1)
    lowest, highest = (0.5, 2.5)
    jitter = jnp.exp(jax.random.uniform(key, (MODEL_WIDTH,), jnp.float32, math.log(0.8), math.log(1.25)))
    return jnp.exp(math.log(lowest) + math.log(highest / lowest) * position) * jitter


def draw_gate_weight(key, part):
    first_key = jax.random.fold_in(key, 11)
    second_key = jax.random.fold_in(key, 23)
    scale = 1.0 / math.sqrt(MODEL_WIDTH)
    entries = jnp.clip(jax.random.normal(first_key, (MODEL_WIDTH, MODEL_WIDTH), jnp.float32), -4.0, 4.0)
    shared = jnp.clip(1.5 * jax.random.normal(second_key, (1, MODEL_WIDTH), jnp.float32), -3.75, 3.75)
    return (scale * (entries + shared)).astype(jnp.bfloat16)


def strengthened(values, own_key, source, target, shards_of, factor):
    owner, partner = [(jnp.arange(values.shape[dim]) // (values.shape[dim] // shards_of)).reshape([-1 if axis == dim else 1 for axis in range(values.ndim)]) for dim in (source, target)]
    chosen = jax.random.permutation(own_key, shards_of)[partner]
    strong = (owner == chosen) | (owner == (partner + shards_of // 2) % shards_of)
    return jnp.where(strong, factor * values, values)


def block_scale(key, dims, pieces, least, top_value):
    factor_of, own = 1.0, jax.random.fold_in(key, 6)
    for axis_at, blocks in pieces:
        steps = jnp.exp(jax.random.uniform(jax.random.fold_in(own, axis_at), (blocks,), jnp.float32, least / len(pieces), top_value / len(pieces)))
        factor_of = factor_of * jnp.repeat(steps, dims[axis_at] // blocks).reshape([-1 if axis == axis_at else 1 for axis in range(len(dims))])
    return factor_of


def scatter_about(rng, extent, spread, bound, pieces=(), kind=jnp.bfloat16):
    result = spread * jax.random.normal(rng, extent, jnp.float32)
    if pieces:
        result = result * block_scale(rng, extent, pieces, -0.22, 0.18)
    return jnp.clip(result, -bound, bound).astype(kind)


def bell_draw_with(own_key, shape, scale, limit, split, heavy, kind=jnp.bfloat16):
    values = scale * jax.random.normal(own_key, shape, jnp.float32)
    if split:
        values = values * block_scale(own_key, shape, split, -0.22, 0.18)
    return jnp.clip(strengthened(values, jax.random.fold_in(own_key, 3), *heavy), -limit, limit).astype(kind)


def setup_inputs(seed: int = 0, part: int = 0) -> dict:
    arg_keys = jax.random.split(jax.random.key(seed), 8)
    own_keys = jax.random.split(jax.random.fold_in(arg_keys[7], part), 8)
    features = scatter_about(own_keys[0], (UTT, FRAMES, MODEL_WIDTH), 1.0, 6.0, ((0, 2), (1, 2), (2, 4)))
    output_gradient = scatter_about(own_keys[1], (UTT, FRAMES, MODEL_WIDTH), 1.0, 6.0, ((0, 2), (1, 2), (2, 4)))
    value_weight = bell_draw_with(arg_keys[2], (MODEL_WIDTH, MODEL_WIDTH), MODEL_WIDTH ** -0.5, 0.109375, ((0, 2), (1, 4)), (1, 0, 4, 2.0))
    gate_weight = draw_gate_weight(jax.random.fold_in(arg_keys[7], 71), part)
    mixer_weight = bell_draw_with(arg_keys[4], (MODEL_WIDTH, MODEL_WIDTH), MODEL_WIDTH ** -0.5, 0.109375, ((0, 2), (1, 4)), (1, 0, 4, 2.0))
    conv_kernel = scatter_about(arg_keys[5], (KERNEL, MODEL_WIDTH), KERNEL ** -0.5, 1.0, ((1, 4),), jnp.float32)
    layer_norm_gain = draw_layer_norm_gain(jax.random.fold_in(arg_keys[7], 71), part)
    return dict(features=features, output_gradient=output_gradient, value_weight=value_weight, gate_weight=gate_weight, mixer_weight=mixer_weight, conv_kernel=conv_kernel, layer_norm_gain=layer_norm_gain)


EPS = 1e-05

def rounded(values):
    return lax.optimization_barrier(values.astype(jnp.bfloat16)).astype(jnp.float32)

def block_products(pairs, row_span):
    width = MODEL_WIDTH // N_COL
    contract_last = (((1,), (1,)), ((), ()))

    def add_block(block, total):
        start = jnp.asarray(block, jnp.int32) * width
        partial_value = jnp.zeros((row_span, MODEL_WIDTH), jnp.float32)
        for left, weights in pairs:
            left_cols = lax.dynamic_slice_in_dim(left, start, width, 1)
            weight_cols = lax.dynamic_slice_in_dim(weights, start, width, 1)
            partial_value = partial_value + lax.dot_general(left_cols, weight_cols, contract_last, preferred_element_type=jnp.float32)
        return total + rounded(partial_value)
    return lax.fori_loop(0, N_COL, add_block, jnp.zeros((row_span, MODEL_WIDTH), jnp.float32))

def weight_grad(left, right):
    total = jnp.zeros((left.shape[2], right.shape[2]), jnp.float32)
    for dp_index in range(N_DP):
        for row_index in range(N_ROW):
            left_block = left[dp_index * UTT_DEV:(dp_index + 1) * UTT_DEV, row_index * TF_DEV:(row_index + 1) * TF_DEV]
            right_block = right[dp_index * UTT_DEV:(dp_index + 1) * UTT_DEV, row_index * TF_DEV:(row_index + 1) * TF_DEV]
            partial_value = lax.dot_general(left_block.reshape(-1, left.shape[2]), right_block.reshape(-1, right.shape[2]), (((0,), (0,)), ((), ())), preferred_element_type=jnp.float32)
            total = total + rounded(partial_value)
    return total

def reference(features, output_gradient, value_weight, gate_weight, mixer_weight, conv_kernel, layer_norm_gain):
    row_span = UTT * FRAMES
    half = KERNEL // 2
    feat_float = features.astype(jnp.float32)
    row_average = lax.optimization_barrier(jnp.mean(feat_float, -1, keepdims=True))
    centered_input = feat_float - row_average
    variance = lax.optimization_barrier(jnp.mean(centered_input * centered_input, -1, keepdims=True))
    inverse_deviation = lax.rsqrt(variance + EPS)
    standardized_input = centered_input * inverse_deviation
    normalized_rows = (standardized_input * layer_norm_gain).astype(jnp.bfloat16)
    normed_rows = normalized_rows.reshape(row_span, MODEL_WIDTH)
    value = jnp.dot(normed_rows, value_weight, preferred_element_type=jnp.float32)
    gate = jnp.dot(normed_rows, gate_weight, preferred_element_type=jnp.float32)
    sig_gate = jax.nn.sigmoid(gate)
    glu = (value * sig_gate).astype(jnp.bfloat16).reshape(UTT, FRAMES, MODEL_WIDTH)
    glu_pad = jnp.pad(glu, ((0, 0), (half, half), (0, 0)))
    conv = jnp.zeros((UTT, FRAMES, MODEL_WIDTH), jnp.float32)
    for kernel_tap in range(KERNEL):
        conv = conv + conv_kernel[kernel_tap] * glu_pad[:, kernel_tap:kernel_tap + FRAMES].astype(jnp.float32)
    sig_conv = jax.nn.sigmoid(conv)
    mixed = (conv * sig_conv).astype(jnp.bfloat16)
    projected = jnp.dot(mixed.reshape(row_span, MODEL_WIDTH), mixer_weight, preferred_element_type=jnp.float32)
    module_out = (feat_float + projected.reshape(UTT, FRAMES, MODEL_WIDTH)).astype(jnp.bfloat16)
    grad_rows = output_gradient.reshape(row_span, MODEL_WIDTH)
    mixed_grad = block_products([(grad_rows, mixer_weight)], row_span).reshape(UTT, FRAMES, MODEL_WIDTH)
    swish_slope = sig_conv * (1.0 + conv * (1.0 - sig_conv))
    conv_grad = (mixed_grad * swish_slope).astype(jnp.bfloat16)
    grad_pad = jnp.pad(conv_grad, ((0, 0), (half, half), (0, 0)))
    glu_grad = jnp.zeros((UTT, FRAMES, MODEL_WIDTH), jnp.float32)
    kernel_rows = []
    for kernel_tap in range(KERNEL):
        back = 2 * half - kernel_tap
        glu_grad = glu_grad + conv_kernel[kernel_tap] * grad_pad[:, back:back + FRAMES].astype(jnp.float32)
        kernel_rows.append(lax.optimization_barrier(jnp.sum(glu_pad[:, kernel_tap:kernel_tap + FRAMES].astype(jnp.float32) * conv_grad.astype(jnp.float32), axis=(0, 1))))
    kernel_grad = jnp.stack(kernel_rows)
    glu_grad = glu_grad.reshape(row_span, MODEL_WIDTH)
    value_grad = (glu_grad * sig_gate).astype(jnp.bfloat16)
    gate_grad = (glu_grad * value * sig_gate * (1.0 - sig_gate)).astype(jnp.bfloat16)
    normalized_gradient = block_products([(value_grad, value_weight), (gate_grad, gate_weight)], row_span).reshape(UTT, FRAMES, MODEL_WIDTH)
    norm_gain_gradient = lax.optimization_barrier(jnp.sum(normalized_gradient * standardized_input, axis=(0, 1)))
    scaled_rows = normalized_gradient * layer_norm_gain
    gradient_mean = lax.optimization_barrier(jnp.mean(scaled_rows, -1, keepdims=True))
    projected_mean = lax.optimization_barrier(jnp.mean(scaled_rows * standardized_input, -1, keepdims=True))
    input_gradient = (output_gradient.astype(jnp.float32) + (scaled_rows - gradient_mean - standardized_input * projected_mean) * inverse_deviation).astype(jnp.bfloat16)
    value_weight_grad = weight_grad(normalized_rows, value_grad.reshape(UTT, FRAMES, MODEL_WIDTH))
    gate_weight_grad = weight_grad(normalized_rows, gate_grad.reshape(UTT, FRAMES, MODEL_WIDTH))
    mixer_weight_grad = weight_grad(mixed, output_gradient)
    return (module_out, input_gradient, value_weight_grad, gate_weight_grad, mixer_weight_grad, kernel_grad, norm_gain_gradient)
```

```python
import functools

import jax
import jax.numpy as jnp
from jax import lax
from jax.experimental import pallas as pl
from jax.experimental.pallas import tpu as pltpu
from jax.sharding import PartitionSpec as P

EPS = 1e-05
CONTRACT_LAST = (((1,), (1,)), ((), ()))
CONTRACT_FIRST = (((0,), (0,)), ((), ()))
BF16 = jnp.bfloat16
F32 = jnp.float32
PARTS = 1
CONV_ROWS = 64


def ring(count, shift):
    return [(i, (i + shift) % count) for i in range(count)]


def by_source(pieces, axis):
    count, me = lax.axis_size(axis), lax.axis_index(axis)
    ordered = []
    for j in range(count):
        back = (me - j) % count
        block = pieces[0]
        for s in range(1, count):
            block = jnp.where(back == s, pieces[s], block)
        ordered.append(block)
    return ordered


def exchange(pick, axis):
    count, me = lax.axis_size(axis), lax.axis_index(axis)
    return [pick(me)] + [
        lax.ppermute(pick((me + s) % count), axis, ring(count, s)) for s in range(1, count)
    ]


def send_sum(pick, axis, dtype):
    count, me = lax.axis_size(axis), lax.axis_index(axis)
    sent = [
        lax.ppermute(pick((me + s) % count).astype(dtype), axis, ring(count, s))
        for s in range(1, count)
    ]
    total = pick(me)
    for piece in sent:
        total = total + piece.astype(F32)
    return total


def sum_over(x, axis):
    pieces = exchange(lambda i: x, axis)
    return sum(pieces[1:], pieces[0])


def conv_body(taps, span, value_ref, value_in_ref, gate_ref, gate_in_ref, grad_ref, kernel_ref,
              mixed_ref, value_grad_ref, gate_grad_ref, taps_ref, glu_pad, grad_pad, partial):
    half = taps // 2
    lead = 16
    lanes = glu_pad.shape[1]
    chunk = CONV_ROWS
    zeros = jnp.zeros((lead, lanes), F32)
    for pad in (glu_pad, grad_pad):
        pad[pl.ds(0, lead)] = zeros
        pad[pl.ds(lead + span, lead)] = zeros
    partial[...] = jnp.zeros_like(partial)

    def rows(i):
        return pl.ds(pl.multiple_of(i * chunk, chunk), chunk)

    def padded(i, shift):
        return pl.ds(i * chunk + (lead + shift), chunk)

    @pl.loop(0, span // chunk)
    def _(i):
        gate = gate_ref[rows(i)] + gate_in_ref[rows(i)]
        value = value_ref[rows(i)] + value_in_ref[rows(i)].astype(F32)
        glu_pad[pl.ds(pl.multiple_of(i * chunk + lead, 8), chunk)] = (
            (value * jax.nn.sigmoid(gate)).astype(BF16).astype(F32)
        )

    @pl.loop(0, span // chunk)
    def _(i):
        conv = jnp.zeros((chunk, lanes), F32)
        for tap in range(taps):
            conv = conv + kernel_ref[pl.ds(tap, 1)] * glu_pad[padded(i, tap - half)]
        sig = jax.nn.sigmoid(conv)
        mixed_ref[rows(i)] = (conv * sig).astype(BF16)
        slope = sig * (1.0 + conv * (1.0 - sig))
        grad = (grad_ref[rows(i)].astype(F32) * slope).astype(BF16).astype(F32)
        grad_pad[pl.ds(pl.multiple_of(i * chunk + lead, 8), chunk)] = grad

    @pl.loop(0, span // chunk)
    def _(i):
        grad = grad_pad[pl.ds(pl.multiple_of(i * chunk + lead, 8), chunk)]
        total = jnp.zeros((chunk, lanes), F32)
        for tap in range(taps):
            total = total + kernel_ref[pl.ds(tap, 1)] * grad_pad[padded(i, half - tap)]
            product = glu_pad[padded(i, tap - half)] * grad
            partial[pl.ds(8 * tap, 8)] += sum(
                product[8 * j : 8 * j + 8] for j in range(chunk // 8)
            )
        gate = gate_ref[rows(i)] + gate_in_ref[rows(i)]
        value = value_ref[rows(i)] + value_in_ref[rows(i)].astype(F32)
        sig = jax.nn.sigmoid(gate)
        value_grad_ref[rows(i)] = (total * sig).astype(BF16)
        gate_grad_ref[rows(i)] = (total * value * sig * (1.0 - sig)).astype(BF16)

    for tap in range(taps):
        taps_ref[pl.ds(tap, 1)] = jnp.sum(partial[pl.ds(8 * tap, 8)], 0, keepdims=True)


def conv_block(value, value_in, gate, gate_in, mixed_grad, kernel, utts):
    cells, narrow = value.shape
    span, taps = cells // utts, kernel.shape[0]
    lanes = 128 if narrow % 128 == 0 else narrow
    tall = pl.BlockSpec((span, lanes), lambda u, j: (u, j))
    short = pl.BlockSpec((taps, lanes), lambda u, j: (0, j))
    work = cells * narrow
    mixed, value_grad, gate_grad, kernel_rows = pl.pallas_call(
        functools.partial(conv_body, taps, span),
        grid=(utts, narrow // lanes),
        in_specs=[tall] * 5 + [short],
        out_specs=[tall] * 3 + [pl.BlockSpec((None, taps, lanes), lambda u, j: (u, 0, j))],
        out_shape=[jax.ShapeDtypeStruct((cells, narrow), BF16)] * 3
        + [jax.ShapeDtypeStruct((utts, taps, narrow), F32)],
        scratch_shapes=[
            pltpu.VMEM((span + 32, lanes), F32),
            pltpu.VMEM((span + 32, lanes), F32),
            pltpu.VMEM((8 * taps, lanes), F32),
        ],
        compiler_params=pltpu.CompilerParams(vmem_limit_bytes=24 << 20),
        cost_estimate=pl.CostEstimate(
            flops=6 * taps * work, bytes_accessed=20 * work, transcendentals=3 * work
        ),
        name="conv_block",
    )(value, value_in, gate, gate_in, mixed_grad, kernel)
    return mixed, value_grad, gate_grad, jnp.sum(kernel_rows, 0)


def shards(
    features, output_gradient, value_weight, gate_weight, mixer_weight, conv_kernel, layer_norm_gain
):
    utts, frames, width = features.shape
    taps = conv_kernel.shape[0]
    half = taps // 2
    model = layer_norm_gain.shape[0]
    n_row, n_col, n_dp = lax.axis_size("row"), lax.axis_size("col"), lax.axis_size("dp")
    row, col, dp = lax.axis_index("row"), lax.axis_index("col"), lax.axis_index("dp")
    per_row = n_col // n_row
    depth = per_row * width
    narrow = width // n_row
    span = n_row * frames
    cells = utts * span
    part = frames // PARTS

    mixer_rows = mixer_weight.reshape(per_row, n_row, narrow, width)
    grad_pieces = exchange(lambda i: output_gradient, "row")
    grad_rows = jnp.stack(by_source(grad_pieces, "row"), axis=1).reshape(cells, width)

    def mixed_part(i):
        rows = lax.dynamic_index_in_dim(mixer_rows, i, 1, keepdims=False)
        return jnp.stack(
            [
                lax.dot_general(
                    grad_rows, rows[p], CONTRACT_LAST, preferred_element_type=F32
                ).astype(BF16)
                for p in range(per_row)
            ]
        )

    mixed_parts = by_source(exchange(mixed_part, "row"), "row")
    mixed_grad = lax.psum_scatter(
        jnp.concatenate(mixed_parts).reshape(n_col * cells, narrow),
        "col",
        scatter_dimension=0,
        tiled=True,
    )

    gain_cols = layer_norm_gain.reshape(n_col, 1, 1, width)
    standard, inverses, crossed = [], [], []
    for i in range(PARTS):
        block = lax.all_gather(features[:, i * part : (i + 1) * part], "col", axis=0).astype(F32)
        mean = jnp.mean(block, (0, 3))[None, :, :, None]
        centered = block - mean
        inverse = lax.rsqrt(jnp.mean(centered * centered, (0, 3)) + EPS)[None, :, :, None]
        xhat = centered * inverse
        standard.append(xhat)
        inverses.append(inverse[0])
        normed_all = (xhat * gain_cols).astype(BF16)

        def channels(j):
            piece = lax.dynamic_slice_in_dim(normed_all, j * per_row, per_row, 0)
            return piece.transpose(1, 2, 0, 3).reshape(utts, part, depth)

        crossed.append(jnp.stack(by_source(exchange(channels, "row"), "row"), axis=1))
    normed = jnp.concatenate(crossed, axis=2).reshape(cells, depth)

    def send_half(x, dtype):
        def columns(i):
            return lax.dynamic_slice_in_dim(x, i * narrow, narrow, 1)

        sent = [
            lax.ppermute(columns((row + s) % n_row).astype(dtype), "row", ring(n_row, s))
            for s in range(1, n_row)
        ]
        return columns(row), sum([p.astype(F32) for p in sent[1:]], sent[0])

    gate_part = jnp.dot(normed, gate_weight, preferred_element_type=F32)
    value_part = jnp.dot(normed, value_weight, preferred_element_type=F32)
    gate, gate_in = send_half(gate_part, F32)
    value, value_in = send_half(value_part, BF16)
    kernel_own = lax.dynamic_slice_in_dim(conv_kernel, row * narrow, narrow, 1)
    mixed, value_grad, gate_grad, kernel_rows = conv_block(
        value, value_in, gate, gate_in, mixed_grad, kernel_own, utts
    )
    mixed = mixed.reshape(utts, span, narrow)
    value_grad, gate_grad = (
        jnp.concatenate(by_source(exchange(lambda i: g, "row"), "row"), axis=1)
        for g in (value_grad, gate_grad)
    )

    value_frames, gate_frames = (
        g.reshape(utts, n_row, PARTS, part, width) for g in (value_grad, gate_grad)
    )
    normed_grads, sums, gain_sums = [], [], []
    for i in range(PARTS):

        def normed_part(j):
            v, g = (
                lax.dynamic_index_in_dim(x[:, :, i], j, 1, keepdims=False).reshape(-1, width)
                for x in (value_frames, gate_frames)
            )
            part_sum = lax.dot_general(
                v, value_weight, CONTRACT_LAST, preferred_element_type=F32
            ) + lax.dot_general(g, gate_weight, CONTRACT_LAST, preferred_element_type=F32)
            part_sum = part_sum.astype(BF16)
            return jnp.stack(
                [part_sum[:, p * width : (p + 1) * width] for p in range(per_row)]
            )

        parts = jnp.concatenate(by_source(exchange(normed_part, "row"), "row"))
        summed = lax.psum_scatter(
            parts.reshape(n_col * utts * part, width), "col", scatter_dimension=0, tiled=True
        )
        normed_grads.append(summed.astype(F32).reshape(utts, part, width))
        wide = parts.astype(F32).reshape(n_col, utts, part, width)
        along = wide * standard[i]
        sums.append(
            jnp.stack([jnp.sum(wide * gain_cols, (0, 3)), jnp.sum(along * gain_cols, (0, 3))])
        )
        gain_sums.append(jnp.sum(along, (1, 2)))
    normed_grad = jnp.concatenate(normed_grads, axis=1)
    sums = sum_over(jnp.concatenate(sums, axis=2), "col")
    gain_sum = sum_over(sum_over(sum(gain_sums), "dp"), "row")
    gain_pieces = exchange(
        lambda j: lax.dynamic_index_in_dim(gain_sum, j, 0, keepdims=False), "col"
    )
    norm_gain_gradient = sum(gain_pieces[1:], gain_pieces[0])

    mixed_gathered = lax.all_gather(mixed, "col", axis=0)
    mixed_pieces = by_source(
        exchange(
            lambda j: lax.dynamic_slice_in_dim(mixed_gathered, j * per_row, per_row, 0), "row"
        ),
        "row",
    )
    mixed_rows = (
        jnp.stack(mixed_pieces, axis=1).transpose(2, 3, 0, 1, 4).reshape(cells, depth)
    )
    projected = jnp.dot(mixed_rows, mixer_weight, preferred_element_type=F32)
    projected = projected.reshape(utts, span, width)
    projected = send_sum(
        lambda j: lax.dynamic_slice_in_dim(projected, j * frames, frames, 1), "row", BF16
    )
    module_out = (features.astype(F32) + projected).astype(BF16)

    share = depth // n_dp

    def spread(x):
        return jnp.concatenate(
            exchange(lambda j: lax.dynamic_slice_in_dim(x, j * share, share, 1), "dp")
        )

    def collect(x):
        return jnp.concatenate(exchange(lambda j: x, "dp"))

    def weight_grad(left, right):
        return lax.dot_general(left, right, CONTRACT_FIRST, preferred_element_type=F32)

    normed_cells = spread(normed)
    value_weight_grad = weight_grad(normed_cells, collect(value_grad))
    gate_weight_grad = weight_grad(normed_cells, collect(gate_grad))
    mixer_weight_grad = weight_grad(spread(mixed_rows), collect(grad_rows))

    kernel_sum = sum_over(kernel_rows, "dp")
    kernel_grad = jnp.concatenate(by_source(exchange(lambda j: kernel_sum, "row"), "row"), axis=1)

    own_standard = jnp.concatenate(
        [lax.dynamic_index_in_dim(x, col, 0, keepdims=False) for x in standard], axis=1
    )
    inverse_own = jnp.concatenate(inverses, axis=1)
    gain_own = lax.dynamic_slice_in_dim(layer_norm_gain, col * width, width, 0)
    scaled = normed_grad * gain_own
    input_gradient = (
        output_gradient.astype(F32)
        + (scaled - sums[0][..., None] / model - own_standard * (sums[1][..., None] / model))
        * inverse_own
    ).astype(BF16)
    return (
        module_out,
        input_gradient,
        value_weight_grad,
        gate_weight_grad,
        mixer_weight_grad,
        kernel_grad,
        norm_gain_gradient,
    )


def solution(mesh):
    placed = (
        P(("groups", "dp"), "row", "col"),
        P(("groups", "dp"), "row", "col"),
        P("row", "col"),
        P("row", "col"),
        P("row", "col"),
        P(None, "col"),
        P(),
    )
    return jax.shard_map(
        shards,
        mesh=mesh,
        in_specs=placed,
        out_specs=(
            P(("groups", "dp"), "row", "col"),
            P(("groups", "dp"), "row", "col"),
            P(("groups", "row", "dp"), "col"),
            P(("groups", "row", "dp"), "col"),
            P(("groups", "row", "dp"), "col"),
            P("groups", "col"),
            P(("groups", "col")),
        ),
        check_vma=False,
    )
```

```python
import functools

import jax
import jax.numpy as jnp
from jax import lax
from jax.experimental import pallas as pl
from jax.experimental.pallas import tpu as pltpu
from jax.sharding import PartitionSpec as P

EPS = 1e-05
CONTRACT_LAST = (((1,), (1,)), ((), ()))
CONTRACT_FIRST = (((0,), (0,)), ((), ()))
BF16 = jnp.bfloat16
F32 = jnp.float32
CONV_ROWS = 64
CONV_VMEM = 56 << 20
NORM_ROWS = 32
BACK_TILE = 512
BACK_VMEM = 40 << 20
NORM_VMEM = 24 << 20
PARTS = 2


def ring(count, shift):
    return [(i, (i + shift) % count) for i in range(count)]


def by_source(pieces, axis):
    count, me = lax.axis_size(axis), lax.axis_index(axis)
    ordered = []
    for j in range(count):
        back = (me - j) % count
        block = pieces[0]
        for s in range(1, count):
            block = jnp.where(back == s, pieces[s], block)
        ordered.append(block)
    return ordered


def exchange(pick, axis):
    count, me = lax.axis_size(axis), lax.axis_index(axis)
    return [pick(me)] + [
        lax.ppermute(pick((me + s) % count), axis, ring(count, s)) for s in range(1, count)
    ]


def after(x, *others):
    return lax.optimization_barrier((x,) + others)[0]


def dot(a, b):
    return jnp.dot(a, b, preferred_element_type=F32)


def dot_last(a, b):
    return lax.dot_general(a, b, CONTRACT_LAST, preferred_element_type=F32)


def sum_over(x, axis):
    pieces = exchange(lambda i: x, axis)
    return sum(pieces[1:], pieces[0])


def conv_body(taps, frames, rows_in, row_ref, *refs):
    parts = [refs[i * rows_in : (i + 1) * rows_in] for i in range(4)]
    grad_ref, kernel_ref, mixed_ref, pair_ref, taps_ref = refs[4 * rows_in : 4 * rows_in + 5]
    glu_pad, grad_pad, partial, value_sum, gate_sum = refs[4 * rows_in + 5 :]
    half = taps // 2
    span = frames * rows_in
    lead = 16
    lanes = glu_pad.shape[1]
    chunk = CONV_ROWS
    per_block = frames // chunk
    row = row_ref[0]
    zeros = jnp.zeros((lead, lanes), F32)
    for pad in (glu_pad, grad_pad):
        pad[pl.ds(0, lead)] = zeros
        pad[pl.ds(lead + span, lead)] = zeros
    partial[...] = jnp.zeros_like(partial)

    def rows(i):
        return pl.ds(pl.multiple_of(i * chunk, chunk), chunk)

    def frame(i):
        block = lax.div(i, per_block)
        place = lax.rem(row - block + rows_in, rows_in)
        return pl.multiple_of(place * frames + (i - block * per_block) * chunk, chunk)

    for k in range(rows_in):
        value_ref, value_in_ref, gate_ref, gate_in_ref = (p[k] for p in parts)

        @pl.loop(0, per_block)
        def _(i, k=k):
            gate = gate_ref[rows(i)] + gate_in_ref[rows(i)]
            value = value_ref[rows(i)] + value_in_ref[rows(i)].astype(F32)
            at = i + k * per_block
            gate_sum[rows(at)] = gate
            value_sum[rows(at)] = value
            glu_pad[pl.ds(pl.multiple_of(frame(at) + lead, 8), chunk)] = (
                (value * jax.nn.sigmoid(gate)).astype(BF16).astype(F32)
            )

    @pl.loop(0, span // chunk)
    def _(i):
        at = frame(i) + lead
        conv = jnp.zeros((chunk, lanes), F32)
        for tap in range(taps):
            conv = conv + kernel_ref[pl.ds(tap, 1)] * glu_pad[pl.ds(at + (tap - half), chunk)]
        sig = jax.nn.sigmoid(conv)
        mixed_ref[rows(i)] = (conv * sig).astype(BF16)
        slope = sig * (1.0 + conv * (1.0 - sig))
        grad = (grad_ref[rows(i)].astype(F32) * slope).astype(BF16).astype(F32)
        grad_pad[pl.ds(pl.multiple_of(at, 8), chunk)] = grad

    @pl.loop(0, span // chunk)
    def _(i):
        at = frame(i) + lead
        grad = grad_pad[pl.ds(pl.multiple_of(at, 8), chunk)]
        total = jnp.zeros((chunk, lanes), F32)
        for tap in range(taps):
            total = total + kernel_ref[pl.ds(tap, 1)] * grad_pad[pl.ds(at + (half - tap), chunk)]
            product = glu_pad[pl.ds(at + (tap - half), chunk)] * grad
            partial[pl.ds(8 * tap, 8)] += sum(
                product[8 * j : 8 * j + 8] for j in range(chunk // 8)
            )
        sig = jax.nn.sigmoid(gate_sum[rows(i)])
        block = lax.div(i, per_block)
        inside = pl.ds(pl.multiple_of((i - block * per_block) * chunk, chunk), chunk)
        pair_ref[block, 0, inside] = (total * sig).astype(BF16)
        pair_ref[block, 1, inside] = (total * value_sum[rows(i)] * sig * (1.0 - sig)).astype(BF16)

    for tap in range(taps):
        taps_ref[pl.ds(tap, 1)] = jnp.sum(partial[pl.ds(8 * tap, 8)], 0, keepdims=True)


def conv_block(row, values, values_in, gates, gates_in, mixed_grad, conv_kernel, frames):
    rows_in = len(values)
    span, narrow = mixed_grad.shape
    taps = conv_kernel.shape[0]
    lanes = 128 if narrow % 128 == 0 else narrow
    steps = narrow // lanes
    if lanes == narrow:
        values, gates, (conv_kernel,) = (
            [lax.dynamic_slice_in_dim(x, row * narrow, narrow, 1) for x in xs]
            for xs in (values, gates, [conv_kernel])
        )

    def at(j, row):
        return (0, j) if lanes == narrow else (0, row[0] * steps + j)

    inner = pl.BlockSpec((frames, lanes), lambda j, row: (0, j))
    outer = pl.BlockSpec((frames, lanes), at)
    tall = pl.BlockSpec((span, lanes), lambda j, row: (0, j))
    work = span * narrow
    return pl.pallas_call(
        functools.partial(conv_body, taps, frames, rows_in),
        grid_spec=pltpu.PrefetchScalarGridSpec(
            num_scalar_prefetch=1,
            grid=(steps,),
            in_specs=[outer] * rows_in
            + [inner] * rows_in
            + [outer] * rows_in
            + [inner] * rows_in
            + [tall, pl.BlockSpec((taps, lanes), at)],
            out_specs=[
                tall,
                pl.BlockSpec((rows_in, 2, frames, lanes), lambda j, row: (0, 0, 0, j)),
                pl.BlockSpec((taps, lanes), lambda j, row: (0, j)),
            ],
            scratch_shapes=[
                pltpu.VMEM((span + 32, lanes), F32),
                pltpu.VMEM((span + 32, lanes), F32),
                pltpu.VMEM((8 * taps, lanes), F32),
                pltpu.VMEM((span, lanes), F32),
                pltpu.VMEM((span, lanes), F32),
            ],
        ),
        out_shape=[
            jax.ShapeDtypeStruct((span, narrow), BF16),
            jax.ShapeDtypeStruct((rows_in, 2, frames, narrow), BF16),
            jax.ShapeDtypeStruct((taps, narrow), F32),
        ],
        compiler_params=pltpu.CompilerParams(vmem_limit_bytes=CONV_VMEM),
        cost_estimate=pl.CostEstimate(
            flops=6 * taps * work, bytes_accessed=20 * work, transcendentals=3 * work
        ),
        name="conv_block",
    )(row.reshape(1), *values, *values_in, *gates, *gates_in, mixed_grad, conv_kernel)


def back_body(value_ref, gate_ref, value_weight_ref, gate_weight_ref, out_ref):
    out_ref[...] = (
        dot_last(value_ref[...], value_weight_ref[...])
        + dot_last(gate_ref[...], gate_weight_ref[...])
    ).astype(BF16)


def back_block(value, gate, value_weight, gate_weight):
    rows, width = value.shape
    depth = value_weight.shape[0]
    tile = BACK_TILE if width % BACK_TILE == 0 else width
    tiles = width // tile
    left = pl.BlockSpec((rows, width), lambda i: (0, 0))
    right = pl.BlockSpec((tile, width), lambda i: (i, 0))
    return pl.pallas_call(
        back_body,
        grid=(depth // tile,),
        in_specs=[left, left, right, right],
        out_specs=pl.BlockSpec((None, rows, tile), lambda i: (i // tiles, 0, i % tiles)),
        out_shape=jax.ShapeDtypeStruct((depth // width, rows, width), BF16),
        compiler_params=pltpu.CompilerParams(vmem_limit_bytes=BACK_VMEM),
        cost_estimate=pl.CostEstimate(
            flops=4 * rows * depth * width,
            bytes_accessed=4 * depth * width + 4 * rows * width + 2 * rows * depth,
            transcendentals=0,
        ),
        name="back_block",
    )(value, gate, value_weight, gate_weight)


def norm_body(per_row, n_row, row_ref, x_ref, gain_ref, *outs):
    n_col, rows, width = x_ref.shape
    mean_ref, inverse_ref = outs[n_row:]
    row = row_ref[0]
    total = sum(x_ref[j].astype(F32) for j in range(n_col))
    mean = jnp.sum(total, -1, keepdims=True) / (n_col * width)
    square = jnp.zeros((rows, width), F32)
    for j in range(n_col):
        centered = x_ref[j].astype(F32) - mean
        square = square + centered * centered
    inverse = lax.rsqrt(jnp.sum(square, -1, keepdims=True) / (n_col * width) + EPS)
    mean_ref[...] = mean
    inverse_ref[...] = inverse
    for s in range(n_row):
        for p in range(per_row):
            j = lax.rem(row + s, n_row) * per_row + p
            xhat = (x_ref[j].astype(F32) - mean) * inverse
            outs[s][:, p * width : (p + 1) * width] = (xhat * gain_ref[j]).astype(BF16)


def norm_block(row, x, gain_cols, n_row):
    n_col, rows, width = x.shape
    per_row = n_col // n_row
    step = NORM_ROWS
    whole = pl.BlockSpec((step, per_row * width), lambda i, row: (i, 0))
    thin = pl.BlockSpec((step, 1), lambda i, row: (i, 0))
    work = n_col * rows * width
    return pl.pallas_call(
        functools.partial(norm_body, per_row, n_row),
        grid_spec=pltpu.PrefetchScalarGridSpec(
            num_scalar_prefetch=1,
            grid=(rows // step,),
            in_specs=[
                pl.BlockSpec((n_col, step, width), lambda i, row: (0, i, 0)),
                pl.BlockSpec((n_col, 1, width), lambda i, row: (0, 0, 0)),
            ],
            out_specs=[whole] * n_row + [thin] * 2,
        ),
        out_shape=[jax.ShapeDtypeStruct((rows, per_row * width), BF16)] * n_row
        + [jax.ShapeDtypeStruct((rows, 1), F32)] * 2,
        compiler_params=pltpu.CompilerParams(vmem_limit_bytes=NORM_VMEM),
        cost_estimate=pl.CostEstimate(
            flops=10 * work, bytes_accessed=4 * work, transcendentals=rows
        ),
        name="norm_block",
    )(row.reshape(1), x, gain_cols)


def shards(
    features, output_gradient, value_weight, gate_weight, mixer_weight, conv_kernel, layer_norm_gain
):
    utts, frames, width = features.shape
    model = layer_norm_gain.shape[0]
    n_row, n_col, n_dp = lax.axis_size("row"), lax.axis_size("col"), lax.axis_size("dp")
    row, col = lax.axis_index("row"), lax.axis_index("col")
    per_row = n_col // n_row
    depth = per_row * width
    narrow = width // n_row
    tokens = utts * frames
    shifts = range(1, n_row)

    def to_row(x, s):
        return lax.ppermute(x, "row", ring(n_row, s))

    def rolled(blocks, s):
        return [blocks[(k - s) % n_row] for k in range(n_row)]

    def placed(pieces):
        buffer = jnp.zeros((n_row,) + pieces[0].shape, pieces[0].dtype)
        for k, piece in enumerate(pieces):
            buffer = lax.dynamic_update_index_in_dim(buffer, piece, (row - k) % n_row, 0)
        return buffer.reshape((-1,) + pieces[0].shape[1:])

    own = features.reshape(tokens, width)
    own_grad = output_gradient.reshape(tokens, width)
    part = tokens // PARTS
    gathered = [
        lax.all_gather(own[i * part : (i + 1) * part], "col", axis=0) for i in range(PARTS)
    ]

    mixer_rows = mixer_weight.reshape(per_row, n_row, narrow, width)
    mixer_of = [
        lax.dynamic_index_in_dim(mixer_rows, (row - k) % n_row, 1, keepdims=False).reshape(
            per_row * narrow, width
        )
        for k in range(n_row)
    ]

    def by_narrow(x):
        return jnp.stack([x[:, p * narrow : (p + 1) * narrow] for p in range(per_row)])

    def mixed_part(rows, s):
        return by_narrow(dot_last(rows, mixer_of[-s % n_row]).astype(BF16))

    grads = [own_grad] + [to_row(own_grad, s) for s in shifts]
    grad_rows = jnp.concatenate(grads)
    mixed_parts = [jnp.concatenate([mixed_part(g, 0) for g in grads], 1)]
    for s in shifts:
        sent = [mixed_part(g, s) for g in grads]
        arrived = [to_row(sent[(k - s) % n_row], s) for k in range(n_row)]
        mixed_parts.append(jnp.concatenate(arrived, 1))
    mixed_parts = jnp.concatenate(by_source(mixed_parts, "row"))

    gain_cols = layer_norm_gain.reshape(n_col, 1, width)
    means, inverses, kept, crossed, sent_out = [], [], [], [], []
    for x in gathered:
        if crossed:
            x = after(x, *crossed[-1])
        *pieces, mean, inverse = norm_block(row, x, gain_cols, n_row)
        kept.append(pieces[0])
        sent_out.append(pieces[1:])
        crossed.append([to_row(x, s) for s, x in zip(shifts, pieces[1:])])
        means.append(mean)
        inverses.append(inverse)
    mean, inverse = jnp.concatenate(means), jnp.concatenate(inverses)
    normed_own = jnp.concatenate(kept)
    normed_in = [jnp.concatenate([c[s - 1] for c in crossed]) for s in shifts]
    normed = jnp.concatenate([normed_own] + normed_in)

    mixed_grad = lax.psum_scatter(
        mixed_parts.reshape(n_col * n_row * tokens, narrow),
        "col",
        scatter_dimension=0,
        tiled=True,
    )

    def columns(x, i):
        return lax.dynamic_slice_in_dim(x, i * narrow, narrow, 1)

    gate_own, value_own = dot(normed_own, gate_weight), dot(normed_own, value_weight)
    rest = jnp.concatenate(normed_in)
    gate_rest, value_rest = dot(rest, gate_weight), dot(rest, value_weight)

    def reduced(first, others, dtype):
        blocks = [first] + [others[k * tokens : (k + 1) * tokens] for k in range(n_row - 1)]
        total = None
        for s in shifts:
            sent = [columns(x, (row + s) % n_row).astype(dtype) for x in blocks]
            sent[0] = after(sent[0], *crossed[-1])
            arrived = [to_row(sent[(k - s) % n_row], s) for k in range(n_row)]
            if total is None:
                total = arrived
            else:
                total = [t.astype(F32) + x.astype(F32) for t, x in zip(total, arrived)]
        return blocks, total

    gate, gate_in = reduced(gate_own, gate_rest, F32)
    value, value_in = reduced(value_own, value_rest, BF16)

    share = depth // n_dp

    def spread(x):
        return jnp.concatenate(
            exchange(lambda j: lax.dynamic_slice_in_dim(x, j * share, share, 1), "dp")
        )

    def collect(x):
        return jnp.concatenate(exchange(lambda j: x, "dp"))

    normed_cells, grad_cells = spread(normed), collect(grad_rows)
    mixed_grad = after(mixed_grad, normed_cells, grad_cells)
    mixed, pair, kernel_rows = conv_block(
        row, value, value_in, gate, gate_in, mixed_grad, conv_kernel, frames
    )

    pair_blocks = [pair[k] for k in range(n_row)]
    first_in, second_in = [], []
    for s in shifts:
        order = rolled(pair_blocks, s)
        first_in.append([to_row(x, s) for x in order[1:]])
    for s in shifts:
        order = rolled(pair_blocks, s)
        second_in.append(to_row(after(order[0], *[x for y in first_in for x in y]), s))
    mixed_all = lax.all_gather(mixed, "col", axis=0)

    pair_kept = [after(x, *[y for z in first_in for y in z]) for x in pair_blocks]

    def wide(i, k):
        pieces = [pair_kept[k]] + [
            second_in[s - 1] if k == 0 else first_in[s - 1][k - 1] for s in shifts
        ]
        return jnp.concatenate(by_source([x[i] for x in pieces], "row"), axis=1)

    value_others = jnp.concatenate([wide(0, k) for k in range(1, n_row)])
    gate_others = jnp.concatenate([wide(1, k) for k in range(1, n_row)])
    part_others = back_block(value_others, gate_others, value_weight, gate_weight)
    part_in = []
    for s in shifts:
        k = n_row - 1 - s
        part_in.append(to_row(part_others[:, k * tokens : (k + 1) * tokens], s))
    second_in = [after(x, part_others) for x in second_in]
    value_mine, gate_mine = wide(0, 0), wide(1, 0)
    part_mine = back_block(value_mine, gate_mine, value_weight, gate_weight)
    def weight_grad(left, right):
        return lax.dot_general(left, right, CONTRACT_FIRST, preferred_element_type=F32)

    value_weight_grad = weight_grad(
        normed_cells, collect(jnp.concatenate([value_mine, value_others]))
    )

    mixed_all = after(mixed_all, value_weight_grad)

    def mixed_piece(j, k):
        return lax.dynamic_slice(
            mixed_all, (j * per_row, k * tokens, 0), (per_row, tokens, narrow)
        )

    mixed_out = [
        jnp.concatenate(
            [mixed_piece((row + s) % n_row, (k - s) % n_row) for k in range(n_row)], axis=1
        )
        for s in shifts
    ]
    part_in = [after(x, *mixed_out) for x in part_in]
    parts = placed([part_mine] + part_in)
    summed = lax.psum_scatter(
        parts.reshape(n_col * tokens, width), "col", scatter_dimension=0, tiled=True
    )

    mixed_in = [to_row(after(x, *part_in), s) for s, x in zip(shifts, mixed_out)]

    def side_by_side(x):
        return jnp.concatenate([x[p] for p in range(per_row)], axis=1)

    mixed_kept = side_by_side(lax.dynamic_slice_in_dim(mixed_all, row * per_row, per_row, 0))
    projected = dot(mixed_kept, mixer_of[0])

    gate_weight_grad = weight_grad(
        after(normed_cells, *part_in), collect(jnp.concatenate([gate_mine, gate_others]))
    )
    parts_wide = after(parts, gate_weight_grad).astype(F32)
    standard = (jnp.concatenate(gathered, axis=1).astype(F32) - mean) * inverse
    along = parts_wide * standard
    sums = jnp.stack([jnp.sum(parts_wide * gain_cols, (0, 2)), jnp.sum(along * gain_cols, (0, 2))])
    gain_sum = jnp.sum(along, 1)
    mixed_blocks = [mixed_kept]
    for s, piece in zip(shifts, mixed_in):
        mixed_blocks.append(side_by_side(after(piece, gate_weight_grad, projected)))
        projected = projected + dot(mixed_blocks[-1], mixer_of[s])
    sums = sum_over(sums, "col")
    gain_sum = sum_over(gain_sum, "dp")
    gain_pieces = exchange(
        lambda j: lax.dynamic_index_in_dim(gain_sum, j, 0, keepdims=False), "col"
    )
    gain_col = sum(gain_pieces[1:], gain_pieces[0])
    norm_gain_gradient = sum_over(after(gain_col, projected), "row")
    projected_blocks = [projected[k * tokens : (k + 1) * tokens] for k in range(n_row)]
    total = own.astype(F32) + projected_blocks[0]
    for s in shifts:
        total = total + to_row(projected_blocks[-s % n_row].astype(BF16), s).astype(F32)
    module_out = total.astype(BF16).reshape(features.shape)

    mixed_sources = by_source(mixed_blocks, "row")
    mixed_rows = jnp.concatenate(
        [
            mixed_sources[h][:, p * narrow : (p + 1) * narrow]
            for p in range(per_row)
            for h in range(n_row)
        ],
        axis=1,
    )
    mixer_weight_grad = weight_grad(spread(mixed_rows), grad_cells)

    kernel_sum = after(sum_over(after(kernel_rows, *part_in), "dp"), projected)
    kernel_grad = jnp.concatenate(by_source(exchange(lambda j: kernel_sum, "row"), "row"), axis=1)

    normed_grad = summed.astype(F32)
    own_standard = (own.astype(F32) - mean) * inverse
    gain_own = lax.dynamic_slice_in_dim(layer_norm_gain, col * width, width, 0)
    scaled = normed_grad * gain_own
    input_gradient = (
        own_grad.astype(F32)
        + (scaled - sums[0][:, None] / model - own_standard * (sums[1][:, None] / model)) * inverse
    )
    input_gradient = input_gradient.astype(BF16).reshape(features.shape)
    return (
        module_out,
        input_gradient,
        value_weight_grad,
        gate_weight_grad,
        mixer_weight_grad,
        kernel_grad,
        norm_gain_gradient,
    )


def solution(mesh):
    placed = (
        P(("groups", "dp"), "row", "col"),
        P(("groups", "dp"), "row", "col"),
        P("row", "col"),
        P("row", "col"),
        P("row", "col"),
        P(None, "col"),
        P(),
    )
    return jax.shard_map(
        shards,
        mesh=mesh,
        in_specs=placed,
        out_specs=(
            P(("groups", "dp"), "row", "col"),
            P(("groups", "dp"), "row", "col"),
            P(("groups", "row", "dp"), "col"),
            P(("groups", "row", "dp"), "col"),
            P(("groups", "row", "dp"), "col"),
            P("groups", "col"),
            P(("groups", "col")),
        ),
        check_vma=False,
    )
```

```python
import functools

import jax
import jax.numpy as jnp
from jax import lax
from jax.experimental import pallas as pl
from jax.experimental.pallas import tpu as pltpu
from jax.sharding import PartitionSpec as P

EPS = 1e-05
CONTRACT_LAST = (((1,), (1,)), ((), ()))
CONTRACT_FIRST = (((0,), (0,)), ((), ()))
BF16 = jnp.bfloat16
F32 = jnp.float32
CONV_ROWS = 64
CONV_VMEM = 56 << 20
NORM_ROWS = 32
BACK_TILE = 512
HALVES = 2
BACK_VMEM = 40 << 20
NORM_VMEM = 24 << 20
PARTS = 2


def ring(count, shift):
    return [(i, (i + shift) % count) for i in range(count)]


def by_source(pieces, axis):
    count, me = lax.axis_size(axis), lax.axis_index(axis)
    ordered = []
    for j in range(count):
        back = (me - j) % count
        block = pieces[0]
        for s in range(1, count):
            block = jnp.where(back == s, pieces[s], block)
        ordered.append(block)
    return ordered


def exchange(pick, axis):
    count, me = lax.axis_size(axis), lax.axis_index(axis)
    return [pick(me)] + [
        lax.ppermute(pick((me + s) % count), axis, ring(count, s)) for s in range(1, count)
    ]


def after(x, *others):
    return lax.optimization_barrier((x,) + others)[0]


def dot(a, b):
    return jnp.dot(a, b, preferred_element_type=F32)


def dot_last(a, b):
    return lax.dot_general(a, b, CONTRACT_LAST, preferred_element_type=F32)


def sum_over(x, axis):
    pieces = exchange(lambda i: x, axis)
    return sum(pieces[1:], pieces[0])


def conv_body(taps, frames, rows_in, carried, row_ref, *refs):
    parts = [refs[i * rows_in : (i + 1) * rows_in] for i in range(4)]
    grad_ref, kernel_ref = refs[4 * rows_in : 4 * rows_in + 2]
    mixed_ref, pair_ref, taps_ref, *scratch = refs[4 * rows_in + 2 + carried :]
    glu_pad, grad_pad, partial, value_sum, gate_sum = scratch
    half = taps // 2
    span = frames * rows_in
    lead = 16
    lanes = glu_pad.shape[1]
    chunk = CONV_ROWS
    per_block = frames // chunk
    row = row_ref[0]
    zeros = jnp.zeros((lead, lanes), F32)
    for pad in (glu_pad, grad_pad):
        pad[pl.ds(0, lead)] = zeros
        pad[pl.ds(lead + span, lead)] = zeros
    partial[...] = jnp.zeros_like(partial)

    def rows(i):
        return pl.ds(pl.multiple_of(i * chunk, chunk), chunk)

    def frame(i):
        block = lax.div(i, per_block)
        place = lax.rem(row - block + rows_in, rows_in)
        return pl.multiple_of(place * frames + (i - block * per_block) * chunk, chunk)

    for k in range(rows_in):
        value_ref, value_in_ref, gate_ref, gate_in_ref = (p[k] for p in parts)

        @pl.loop(0, per_block)
        def _(i, k=k):
            gate = gate_ref[rows(i)] + gate_in_ref[rows(i)]
            value = value_ref[rows(i)] + value_in_ref[rows(i)].astype(F32)
            at = i + k * per_block
            gate_sum[rows(at)] = gate
            value_sum[rows(at)] = value
            glu_pad[pl.ds(pl.multiple_of(frame(at) + lead, 8), chunk)] = (
                (value * jax.nn.sigmoid(gate)).astype(BF16).astype(F32)
            )

    @pl.loop(0, span // chunk)
    def _(i):
        at = frame(i) + lead
        conv = jnp.zeros((chunk, lanes), F32)
        for tap in range(taps):
            conv = conv + kernel_ref[pl.ds(tap, 1)] * glu_pad[pl.ds(at + (tap - half), chunk)]
        sig = jax.nn.sigmoid(conv)
        mixed_ref[rows(i)] = (conv * sig).astype(BF16)
        slope = sig * (1.0 + conv * (1.0 - sig))
        grad = (grad_ref[rows(i)].astype(F32) * slope).astype(BF16).astype(F32)
        grad_pad[pl.ds(pl.multiple_of(at, 8), chunk)] = grad

    @pl.loop(0, span // chunk)
    def _(i):
        at = frame(i) + lead
        grad = grad_pad[pl.ds(pl.multiple_of(at, 8), chunk)]
        total = jnp.zeros((chunk, lanes), F32)
        for tap in range(taps):
            total = total + kernel_ref[pl.ds(tap, 1)] * grad_pad[pl.ds(at + (half - tap), chunk)]
            product = glu_pad[pl.ds(at + (tap - half), chunk)] * grad
            partial[pl.ds(8 * tap, 8)] += sum(
                product[8 * j : 8 * j + 8] for j in range(chunk // 8)
            )
        sig = jax.nn.sigmoid(gate_sum[rows(i)])
        block = lax.div(i, per_block)
        inside = pl.ds(pl.multiple_of((i - block * per_block) * chunk, chunk), chunk)
        pair_ref[block, 0, inside] = (total * sig).astype(BF16)
        pair_ref[block, 1, inside] = (total * value_sum[rows(i)] * sig * (1.0 - sig)).astype(BF16)

    for tap in range(taps):
        taps_ref[pl.ds(tap, 1)] = jnp.sum(partial[pl.ds(8 * tap, 8)], 0, keepdims=True)


def conv_block(
    row, values, values_in, gates, gates_in, mixed_grad, conv_kernel, frames, count, which, before
):
    rows_in = len(values)
    span, whole = mixed_grad.shape
    narrow = whole // count
    taps = conv_kernel.shape[0]
    lanes = 128 if narrow % 128 == 0 else narrow
    steps = narrow // lanes
    first = which * steps
    if lanes == narrow:
        values, gates, (conv_kernel,) = (
            [lax.dynamic_slice_in_dim(x, row * narrow, narrow, 1) for x in xs]
            for xs in (values, gates, [conv_kernel])
        )

    def at(j, row):
        return (0, j) if lanes == narrow else (0, row[0] * (count * steps) + (first + j))

    inner = pl.BlockSpec((frames, lanes), lambda j, row: (0, j))
    outer = pl.BlockSpec((frames, lanes), at)
    tall = pl.BlockSpec((span, lanes), lambda j, row: (0, first + j))
    work = span * narrow
    return pl.pallas_call(
        functools.partial(conv_body, taps, frames, rows_in, len(before)),
        grid_spec=pltpu.PrefetchScalarGridSpec(
            num_scalar_prefetch=1,
            grid=(steps,),
            in_specs=[outer] * rows_in
            + [inner] * rows_in
            + [outer] * rows_in
            + [inner] * rows_in
            + [tall, pl.BlockSpec((taps, lanes), at)]
            + [pl.BlockSpec(memory_space=pl.ANY)] * len(before),
            out_specs=[
                tall,
                pl.BlockSpec((rows_in, 2, frames, lanes), lambda j, row: (0, 0, 0, first + j)),
                pl.BlockSpec((taps, lanes), lambda j, row: (0, first + j)),
            ],
            scratch_shapes=[
                pltpu.VMEM((span + 32, lanes), F32),
                pltpu.VMEM((span + 32, lanes), F32),
                pltpu.VMEM((8 * taps, lanes), F32),
                pltpu.VMEM((span, lanes), F32),
                pltpu.VMEM((span, lanes), F32),
            ],
        ),
        out_shape=[
            jax.ShapeDtypeStruct((span, whole), BF16),
            jax.ShapeDtypeStruct((rows_in, 2, frames, whole), BF16),
            jax.ShapeDtypeStruct((taps, whole), F32),
        ],
        input_output_aliases={4 * rows_in + 3 + i: i for i in range(len(before))},
        compiler_params=pltpu.CompilerParams(vmem_limit_bytes=CONV_VMEM),
        cost_estimate=pl.CostEstimate(
            flops=6 * taps * work, bytes_accessed=20 * work, transcendentals=3 * work
        ),
        name="conv_block",
    )(row.reshape(1), *values, *values_in, *gates, *gates_in, mixed_grad, conv_kernel, *before)


def back_body(value_ref, gate_ref, value_weight_ref, gate_weight_ref, out_ref):
    out_ref[...] = (
        dot_last(value_ref[...], value_weight_ref[...])
        + dot_last(gate_ref[...], gate_weight_ref[...])
    ).astype(BF16)


def back_block(value, gate, value_weight, gate_weight):
    rows, width = value.shape
    depth = value_weight.shape[0]
    tile = BACK_TILE if width % BACK_TILE == 0 else width
    tiles = width // tile
    left = pl.BlockSpec((rows, width), lambda i: (0, 0))
    right = pl.BlockSpec((tile, width), lambda i: (i, 0))
    return pl.pallas_call(
        back_body,
        grid=(depth // tile,),
        in_specs=[left, left, right, right],
        out_specs=pl.BlockSpec((None, rows, tile), lambda i: (i // tiles, 0, i % tiles)),
        out_shape=jax.ShapeDtypeStruct((depth // width, rows, width), BF16),
        compiler_params=pltpu.CompilerParams(vmem_limit_bytes=BACK_VMEM),
        cost_estimate=pl.CostEstimate(
            flops=4 * rows * depth * width,
            bytes_accessed=4 * depth * width + 4 * rows * width + 2 * rows * depth,
            transcendentals=0,
        ),
        name="back_block",
    )(value, gate, value_weight, gate_weight)


def norm_body(per_row, n_row, row_ref, x_ref, gain_ref, *outs):
    n_col, rows, width = x_ref.shape
    mean_ref, inverse_ref = outs[n_row:]
    row = row_ref[0]
    total = sum(x_ref[j].astype(F32) for j in range(n_col))
    mean = jnp.sum(total, -1, keepdims=True) / (n_col * width)
    square = jnp.zeros((rows, width), F32)
    for j in range(n_col):
        centered = x_ref[j].astype(F32) - mean
        square = square + centered * centered
    inverse = lax.rsqrt(jnp.sum(square, -1, keepdims=True) / (n_col * width) + EPS)
    mean_ref[...] = mean
    inverse_ref[...] = inverse
    for s in range(n_row):
        for p in range(per_row):
            j = lax.rem(row + s, n_row) * per_row + p
            xhat = (x_ref[j].astype(F32) - mean) * inverse
            outs[s][:, p * width : (p + 1) * width] = (xhat * gain_ref[j]).astype(BF16)


def norm_block(row, x, gain_cols, n_row):
    n_col, rows, width = x.shape
    per_row = n_col // n_row
    step = NORM_ROWS
    whole = pl.BlockSpec((step, per_row * width), lambda i, row: (i, 0))
    thin = pl.BlockSpec((step, 1), lambda i, row: (i, 0))
    work = n_col * rows * width
    return pl.pallas_call(
        functools.partial(norm_body, per_row, n_row),
        grid_spec=pltpu.PrefetchScalarGridSpec(
            num_scalar_prefetch=1,
            grid=(rows // step,),
            in_specs=[
                pl.BlockSpec((n_col, step, width), lambda i, row: (0, i, 0)),
                pl.BlockSpec((n_col, 1, width), lambda i, row: (0, 0, 0)),
            ],
            out_specs=[whole] * n_row + [thin] * 2,
        ),
        out_shape=[jax.ShapeDtypeStruct((rows, per_row * width), BF16)] * n_row
        + [jax.ShapeDtypeStruct((rows, 1), F32)] * 2,
        compiler_params=pltpu.CompilerParams(vmem_limit_bytes=NORM_VMEM),
        cost_estimate=pl.CostEstimate(
            flops=10 * work, bytes_accessed=4 * work, transcendentals=rows
        ),
        name="norm_block",
    )(row.reshape(1), x, gain_cols)


def shards(
    features, output_gradient, value_weight, gate_weight, mixer_weight, conv_kernel, layer_norm_gain
):
    utts, frames, width = features.shape
    model = layer_norm_gain.shape[0]
    n_row, n_col, n_dp = lax.axis_size("row"), lax.axis_size("col"), lax.axis_size("dp")
    row, col = lax.axis_index("row"), lax.axis_index("col")
    per_row = n_col // n_row
    depth = per_row * width
    narrow = width // n_row
    tokens = utts * frames
    shifts = range(1, n_row)

    def to_row(x, s):
        return lax.ppermute(x, "row", ring(n_row, s))

    def rolled(blocks, s):
        return [blocks[(k - s) % n_row] for k in range(n_row)]

    def placed(pieces):
        buffer = jnp.zeros((n_row,) + pieces[0].shape, pieces[0].dtype)
        for k, piece in enumerate(pieces):
            buffer = lax.dynamic_update_index_in_dim(buffer, piece, (row - k) % n_row, 0)
        return buffer.reshape((-1,) + pieces[0].shape[1:])

    own = features.reshape(tokens, width)
    own_grad = output_gradient.reshape(tokens, width)
    part = tokens // PARTS
    gathered = [
        lax.all_gather(own[i * part : (i + 1) * part], "col", axis=0) for i in range(PARTS)
    ]

    mixer_rows = mixer_weight.reshape(per_row, n_row, narrow, width)
    mixer_of = [
        lax.dynamic_index_in_dim(mixer_rows, (row - k) % n_row, 1, keepdims=False).reshape(
            per_row * narrow, width
        )
        for k in range(n_row)
    ]

    def by_narrow(x):
        return jnp.stack([x[:, p * narrow : (p + 1) * narrow] for p in range(per_row)])

    def mixed_part(rows, s):
        return by_narrow(dot_last(rows, mixer_of[-s % n_row]).astype(BF16))

    grads = [own_grad] + [to_row(own_grad, s) for s in shifts]
    grad_rows = jnp.concatenate(grads)
    mixed_parts = [jnp.concatenate([mixed_part(g, 0) for g in grads], 1)]
    for s in shifts:
        sent = [mixed_part(g, s) for g in grads]
        arrived = [to_row(sent[(k - s) % n_row], s) for k in range(n_row)]
        mixed_parts.append(jnp.concatenate(arrived, 1))
    mixed_parts = jnp.concatenate(by_source(mixed_parts, "row"))

    gain_cols = layer_norm_gain.reshape(n_col, 1, width)
    means, inverses, kept, crossed, sent_out = [], [], [], [], []
    for x in gathered:
        if crossed:
            x = after(x, *crossed[-1])
        *pieces, mean, inverse = norm_block(row, x, gain_cols, n_row)
        kept.append(pieces[0])
        sent_out.append(pieces[1:])
        crossed.append([to_row(x, s) for s, x in zip(shifts, pieces[1:])])
        means.append(mean)
        inverses.append(inverse)
    mean, inverse = jnp.concatenate(means), jnp.concatenate(inverses)
    normed_own = jnp.concatenate(kept)
    normed_in = [jnp.concatenate([c[s - 1] for c in crossed]) for s in shifts]
    normed = jnp.concatenate([normed_own] + normed_in)

    mixed_grad = lax.psum_scatter(
        mixed_parts.reshape(n_col * n_row * tokens, narrow),
        "col",
        scatter_dimension=0,
        tiled=True,
    )

    count = HALVES if narrow % (HALVES * 128) == 0 else 1
    piece = narrow // count
    gate_own, value_own = dot(normed_own, gate_weight), dot(normed_own, value_weight)
    rest = jnp.concatenate(normed_in)
    gate_rest, value_rest = dot(rest, gate_weight), dot(rest, value_weight)

    def blocks_of(first, others):
        return [first] + [others[k * tokens : (k + 1) * tokens] for k in range(n_row - 1)]

    def reduced(blocks, q, dtype, *others):
        total = None
        for s in shifts:
            start = ((row + s) % n_row) * narrow + q * piece
            sent = [
                after(lax.dynamic_slice_in_dim(x, start, piece, 1).astype(dtype), *others)
                for x in blocks
            ]
            arrived = [to_row(sent[(k - s) % n_row], s) for k in range(n_row)]
            if total is None:
                total = arrived
            else:
                total = [t.astype(F32) + x.astype(F32) for t, x in zip(total, arrived)]
        return total

    gate, value = blocks_of(gate_own, gate_rest), blocks_of(value_own, value_rest)
    gate_in, value_in = [], []
    for q in range(count):
        before = gate_in[-1] + value_in[-1] if q else []
        gate_in.append(reduced(gate, q, F32, *before))
        value_in.append(reduced(value, q, BF16, *before))

    share = depth // n_dp

    def spread(x):
        return jnp.concatenate(
            exchange(lambda j: lax.dynamic_slice_in_dim(x, j * share, share, 1), "dp")
        )

    def collect(x):
        return jnp.concatenate(exchange(lambda j: x, "dp"))

    normed_cells, grad_cells = spread(normed), collect(grad_rows)
    mixed_grad = after(mixed_grad, normed_cells, grad_cells)
    done = []
    for q in range(count):
        here = [[after(x, *done) for x in y[q]] for y in (value_in, gate_in)]
        done = conv_block(
            row, value, here[0], gate, here[1], mixed_grad, conv_kernel, frames, count, q, done
        )
    mixed, pair, kernel_rows = done

    pair_blocks = [pair[k] for k in range(n_row)]
    first_in, second_in = [], []
    for s in shifts:
        order = rolled(pair_blocks, s)
        first_in.append([to_row(x, s) for x in order[1:]])
    for s in shifts:
        order = rolled(pair_blocks, s)
        second_in.append(to_row(after(order[0], *[x for y in first_in for x in y]), s))
    mixed_all = lax.all_gather(mixed, "col", axis=0)

    pair_kept = [after(x, *[y for z in first_in for y in z]) for x in pair_blocks]

    def wide(i, k):
        pieces = [pair_kept[k]] + [
            second_in[s - 1] if k == 0 else first_in[s - 1][k - 1] for s in shifts
        ]
        return jnp.concatenate(by_source([x[i] for x in pieces], "row"), axis=1)

    value_others = jnp.concatenate([wide(0, k) for k in range(1, n_row)])
    gate_others = jnp.concatenate([wide(1, k) for k in range(1, n_row)])
    part_others = back_block(value_others, gate_others, value_weight, gate_weight)
    part_in = []
    for s in shifts:
        k = n_row - 1 - s
        part_in.append(to_row(part_others[:, k * tokens : (k + 1) * tokens], s))
    second_in = [after(x, part_others) for x in second_in]
    value_mine, gate_mine = wide(0, 0), wide(1, 0)
    part_mine = back_block(value_mine, gate_mine, value_weight, gate_weight)
    def weight_grad(left, right):
        return lax.dot_general(left, right, CONTRACT_FIRST, preferred_element_type=F32)

    value_weight_grad = weight_grad(
        normed_cells, collect(jnp.concatenate([value_mine, value_others]))
    )

    mixed_all = after(mixed_all, value_weight_grad)

    def mixed_piece(j, k):
        return lax.dynamic_slice(
            mixed_all, (j * per_row, k * tokens, 0), (per_row, tokens, narrow)
        )

    mixed_out = [
        jnp.concatenate(
            [mixed_piece((row + s) % n_row, (k - s) % n_row) for k in range(n_row)], axis=1
        )
        for s in shifts
    ]
    part_in = [after(x, *mixed_out) for x in part_in]
    parts = placed([part_mine] + part_in)
    summed = lax.psum_scatter(
        parts.reshape(n_col * tokens, width), "col", scatter_dimension=0, tiled=True
    )

    mixed_in = [to_row(after(x, *part_in), s) for s, x in zip(shifts, mixed_out)]

    def side_by_side(x):
        return jnp.concatenate([x[p] for p in range(per_row)], axis=1)

    mixed_kept = side_by_side(lax.dynamic_slice_in_dim(mixed_all, row * per_row, per_row, 0))
    projected = dot(mixed_kept, mixer_of[0])

    gate_weight_grad = weight_grad(
        after(normed_cells, *part_in), collect(jnp.concatenate([gate_mine, gate_others]))
    )
    parts_wide = after(parts, gate_weight_grad).astype(F32)
    standard = (jnp.concatenate(gathered, axis=1).astype(F32) - mean) * inverse
    along = parts_wide * standard
    sums = jnp.stack([jnp.sum(parts_wide * gain_cols, (0, 2)), jnp.sum(along * gain_cols, (0, 2))])
    gain_sum = jnp.sum(along, 1)
    mixed_blocks = [mixed_kept]
    for s, piece in zip(shifts, mixed_in):
        mixed_blocks.append(side_by_side(after(piece, gate_weight_grad, projected)))
        projected = projected + dot(mixed_blocks[-1], mixer_of[s])
    sums = sum_over(sums, "col")
    gain_sum = sum_over(gain_sum, "dp")
    gain_pieces = exchange(
        lambda j: lax.dynamic_index_in_dim(gain_sum, j, 0, keepdims=False), "col"
    )
    gain_col = sum(gain_pieces[1:], gain_pieces[0])
    norm_gain_gradient = sum_over(after(gain_col, projected), "row")
    projected_blocks = [projected[k * tokens : (k + 1) * tokens] for k in range(n_row)]
    total = own.astype(F32) + projected_blocks[0]
    for s in shifts:
        total = total + to_row(projected_blocks[-s % n_row].astype(BF16), s).astype(F32)
    module_out = total.astype(BF16).reshape(features.shape)

    mixed_sources = by_source(mixed_blocks, "row")
    mixed_rows = jnp.concatenate(
        [
            mixed_sources[h][:, p * narrow : (p + 1) * narrow]
            for p in range(per_row)
            for h in range(n_row)
        ],
        axis=1,
    )
    mixer_weight_grad = weight_grad(spread(mixed_rows), grad_cells)

    kernel_sum = after(sum_over(after(kernel_rows, *part_in), "dp"), projected)
    kernel_grad = jnp.concatenate(by_source(exchange(lambda j: kernel_sum, "row"), "row"), axis=1)

    normed_grad = summed.astype(F32)
    own_standard = (own.astype(F32) - mean) * inverse
    gain_own = lax.dynamic_slice_in_dim(layer_norm_gain, col * width, width, 0)
    scaled = normed_grad * gain_own
    input_gradient = (
        own_grad.astype(F32)
        + (scaled - sums[0][:, None] / model - own_standard * (sums[1][:, None] / model)) * inverse
    )
    input_gradient = input_gradient.astype(BF16).reshape(features.shape)
    return (
        module_out,
        input_gradient,
        value_weight_grad,
        gate_weight_grad,
        mixer_weight_grad,
        kernel_grad,
        norm_gain_gradient,
    )


def solution(mesh):
    placed = (
        P(("groups", "dp"), "row", "col"),
        P(("groups", "dp"), "row", "col"),
        P("row", "col"),
        P("row", "col"),
        P("row", "col"),
        P(None, "col"),
        P(),
    )
    return jax.shard_map(
        shards,
        mesh=mesh,
        in_specs=placed,
        out_specs=(
            P(("groups", "dp"), "row", "col"),
            P(("groups", "dp"), "row", "col"),
            P(("groups", "row", "dp"), "col"),
            P(("groups", "row", "dp"), "col"),
            P(("groups", "row", "dp"), "col"),
            P("groups", "col"),
            P(("groups", "col")),
        ),
        check_vma=False,
    )
```

```python
import functools

import jax
import jax.numpy as jnp
from jax import lax
from jax.experimental import pallas as pl
from jax.experimental.pallas import tpu as pltpu
from jax.sharding import PartitionSpec as P

EPS = 1e-05
CONTRACT_LAST = (((1,), (1,)), ((), ()))
CONTRACT_FIRST = (((0,), (0,)), ((), ()))
BF16 = jnp.bfloat16
F32 = jnp.float32
CONV_ROWS = 64
CONV_VMEM = 56 << 20
NORM_ROWS = 32
BACK_TILE = 512
HALVES = 2
BACK_VMEM = 40 << 20
NORM_VMEM = 24 << 20
PARTS = 2


def ring(count, shift):
    return [(i, (i + shift) % count) for i in range(count)]


def by_source(pieces, axis):
    count, me = lax.axis_size(axis), lax.axis_index(axis)
    ordered = []
    for j in range(count):
        back = (me - j) % count
        block = pieces[0]
        for s in range(1, count):
            block = jnp.where(back == s, pieces[s], block)
        ordered.append(block)
    return ordered


def exchange(pick, axis):
    count, me = lax.axis_size(axis), lax.axis_index(axis)
    return [pick(me)] + [
        lax.ppermute(pick((me + s) % count), axis, ring(count, s)) for s in range(1, count)
    ]


def after(x, *others):
    return lax.optimization_barrier((x,) + others)[0]


def dot(a, b):
    return jnp.dot(a, b, preferred_element_type=F32)


def dot_last(a, b):
    return lax.dot_general(a, b, CONTRACT_LAST, preferred_element_type=F32)


def sum_over(x, axis):
    pieces = exchange(lambda i: x, axis)
    return sum(pieces[1:], pieces[0])


def conv_body(taps, frames, rows_in, carried, row_ref, *refs):
    parts = [refs[i * rows_in : (i + 1) * rows_in] for i in range(4)]
    grad_ref, kernel_ref = refs[4 * rows_in : 4 * rows_in + 2]
    mixed_ref, pair_ref, taps_ref, *scratch = refs[4 * rows_in + 2 + carried :]
    glu_pad, grad_pad, partial, value_sum, gate_sum = scratch
    half = taps // 2
    span = frames * rows_in
    lead = 16
    lanes = glu_pad.shape[1]
    chunk = CONV_ROWS
    per_block = frames // chunk
    row = row_ref[0]
    zeros = jnp.zeros((lead, lanes), F32)
    for pad in (glu_pad, grad_pad):
        pad[pl.ds(0, lead)] = zeros
        pad[pl.ds(lead + span, lead)] = zeros
    partial[...] = jnp.zeros_like(partial)

    def rows(i):
        return pl.ds(pl.multiple_of(i * chunk, chunk), chunk)

    def frame(i):
        block = lax.div(i, per_block)
        place = lax.rem(row - block + rows_in, rows_in)
        return pl.multiple_of(place * frames + (i - block * per_block) * chunk, chunk)

    for k in range(rows_in):
        value_ref, value_in_ref, gate_ref, gate_in_ref = (p[k] for p in parts)

        @pl.loop(0, per_block)
        def _(i, k=k):
            gate = gate_ref[rows(i)] + gate_in_ref[rows(i)]
            value = value_ref[rows(i)] + value_in_ref[rows(i)].astype(F32)
            at = i + k * per_block
            gate_sum[rows(at)] = gate
            value_sum[rows(at)] = value
            glu_pad[pl.ds(pl.multiple_of(frame(at) + lead, 8), chunk)] = (
                (value * jax.nn.sigmoid(gate)).astype(BF16).astype(F32)
            )

    @pl.loop(0, span // chunk)
    def _(i):
        at = frame(i) + lead
        conv = jnp.zeros((chunk, lanes), F32)
        for tap in range(taps):
            conv = conv + kernel_ref[pl.ds(tap, 1)] * glu_pad[pl.ds(at + (tap - half), chunk)]
        sig = jax.nn.sigmoid(conv)
        mixed_ref[rows(i)] = (conv * sig).astype(BF16)
        slope = sig * (1.0 + conv * (1.0 - sig))
        grad = (grad_ref[rows(i)].astype(F32) * slope).astype(BF16).astype(F32)
        grad_pad[pl.ds(pl.multiple_of(at, 8), chunk)] = grad

    @pl.loop(0, span // chunk)
    def _(i):
        at = frame(i) + lead
        grad = grad_pad[pl.ds(pl.multiple_of(at, 8), chunk)]
        total = jnp.zeros((chunk, lanes), F32)
        for tap in range(taps):
            total = total + kernel_ref[pl.ds(tap, 1)] * grad_pad[pl.ds(at + (half - tap), chunk)]
            product = glu_pad[pl.ds(at + (tap - half), chunk)] * grad
            partial[pl.ds(8 * tap, 8)] += sum(
                product[8 * j : 8 * j + 8] for j in range(chunk // 8)
            )
        sig = jax.nn.sigmoid(gate_sum[rows(i)])
        block = lax.div(i, per_block)
        inside = pl.ds(pl.multiple_of((i - block * per_block) * chunk, chunk), chunk)
        pair_ref[block, 0, inside] = (total * sig).astype(BF16)
        pair_ref[block, 1, inside] = (total * value_sum[rows(i)] * sig * (1.0 - sig)).astype(BF16)

    for tap in range(taps):
        taps_ref[pl.ds(tap, 1)] = jnp.sum(partial[pl.ds(8 * tap, 8)], 0, keepdims=True)


def conv_block(
    row, values, values_in, gates, gates_in, mixed_grad, conv_kernel, frames, count, which, before
):
    rows_in = len(values)
    span, whole = mixed_grad.shape
    narrow = whole // count
    taps = conv_kernel.shape[0]
    lanes = 128 if narrow % 128 == 0 else narrow
    steps = narrow // lanes
    first = which * steps
    if lanes == narrow:
        values, gates, (conv_kernel,) = (
            [lax.dynamic_slice_in_dim(x, row * narrow, narrow, 1) for x in xs]
            for xs in (values, gates, [conv_kernel])
        )

    def at(j, row):
        return (0, j) if lanes == narrow else (0, row[0] * (count * steps) + (first + j))

    inner = pl.BlockSpec((frames, lanes), lambda j, row: (0, j))
    outer = pl.BlockSpec((frames, lanes), at)
    tall = pl.BlockSpec((span, lanes), lambda j, row: (0, first + j))
    work = span * narrow
    return pl.pallas_call(
        functools.partial(conv_body, taps, frames, rows_in, len(before)),
        grid_spec=pltpu.PrefetchScalarGridSpec(
            num_scalar_prefetch=1,
            grid=(steps,),
            in_specs=[outer] * rows_in
            + [inner] * rows_in
            + [outer] * rows_in
            + [inner] * rows_in
            + [tall, pl.BlockSpec((taps, lanes), at)]
            + [pl.BlockSpec(memory_space=pl.ANY)] * len(before),
            out_specs=[
                tall,
                pl.BlockSpec((rows_in, 2, frames, lanes), lambda j, row: (0, 0, 0, first + j)),
                pl.BlockSpec((taps, lanes), lambda j, row: (0, first + j)),
            ],
            scratch_shapes=[
                pltpu.VMEM((span + 32, lanes), F32),
                pltpu.VMEM((span + 32, lanes), F32),
                pltpu.VMEM((8 * taps, lanes), F32),
                pltpu.VMEM((span, lanes), F32),
                pltpu.VMEM((span, lanes), F32),
            ],
        ),
        out_shape=[
            jax.ShapeDtypeStruct((span, whole), BF16),
            jax.ShapeDtypeStruct((rows_in, 2, frames, whole), BF16),
            jax.ShapeDtypeStruct((taps, whole), F32),
        ],
        input_output_aliases={4 * rows_in + 3 + i: i for i in range(len(before))},
        compiler_params=pltpu.CompilerParams(vmem_limit_bytes=CONV_VMEM),
        cost_estimate=pl.CostEstimate(
            flops=6 * taps * work, bytes_accessed=20 * work, transcendentals=3 * work
        ),
        name="conv_block",
    )(row.reshape(1), *values, *values_in, *gates, *gates_in, mixed_grad, conv_kernel, *before)


def back_body(value_ref, gate_ref, value_weight_ref, gate_weight_ref, out_ref):
    out_ref[...] = (
        dot_last(value_ref[...], value_weight_ref[...])
        + dot_last(gate_ref[...], gate_weight_ref[...])
    ).astype(BF16)


def back_block(value, gate, value_weight, gate_weight):
    rows, width = value.shape
    depth = value_weight.shape[0]
    tile = BACK_TILE if width % BACK_TILE == 0 else width
    tiles = width // tile
    left = pl.BlockSpec((rows, width), lambda i: (0, 0))
    right = pl.BlockSpec((tile, width), lambda i: (i, 0))
    return pl.pallas_call(
        back_body,
        grid=(depth // tile,),
        in_specs=[left, left, right, right],
        out_specs=pl.BlockSpec((None, rows, tile), lambda i: (i // tiles, 0, i % tiles)),
        out_shape=jax.ShapeDtypeStruct((depth // width, rows, width), BF16),
        compiler_params=pltpu.CompilerParams(vmem_limit_bytes=BACK_VMEM),
        cost_estimate=pl.CostEstimate(
            flops=4 * rows * depth * width,
            bytes_accessed=4 * depth * width + 4 * rows * width + 2 * rows * depth,
            transcendentals=0,
        ),
        name="back_block",
    )(value, gate, value_weight, gate_weight)


def norm_body(per_row, n_row, row_ref, x_ref, gain_ref, *outs):
    n_col, rows, width = x_ref.shape
    mean_ref, inverse_ref = outs[n_row:]
    row = row_ref[0]
    total = sum(x_ref[j].astype(F32) for j in range(n_col))
    mean = jnp.sum(total, -1, keepdims=True) / (n_col * width)
    square = jnp.zeros((rows, width), F32)
    for j in range(n_col):
        centered = x_ref[j].astype(F32) - mean
        square = square + centered * centered
    inverse = lax.rsqrt(jnp.sum(square, -1, keepdims=True) / (n_col * width) + EPS)
    mean_ref[...] = mean
    inverse_ref[...] = inverse
    for s in range(n_row):
        for p in range(per_row):
            j = lax.rem(row + s, n_row) * per_row + p
            xhat = (x_ref[j].astype(F32) - mean) * inverse
            outs[s][:, p * width : (p + 1) * width] = (xhat * gain_ref[j]).astype(BF16)


def norm_block(row, x, gain_cols, n_row):
    n_col, rows, width = x.shape
    per_row = n_col // n_row
    step = NORM_ROWS
    whole = pl.BlockSpec((step, per_row * width), lambda i, row: (i, 0))
    thin = pl.BlockSpec((step, 1), lambda i, row: (i, 0))
    work = n_col * rows * width
    return pl.pallas_call(
        functools.partial(norm_body, per_row, n_row),
        grid_spec=pltpu.PrefetchScalarGridSpec(
            num_scalar_prefetch=1,
            grid=(rows // step,),
            in_specs=[
                pl.BlockSpec((n_col, step, width), lambda i, row: (0, i, 0)),
                pl.BlockSpec((n_col, 1, width), lambda i, row: (0, 0, 0)),
            ],
            out_specs=[whole] * n_row + [thin] * 2,
        ),
        out_shape=[jax.ShapeDtypeStruct((rows, per_row * width), BF16)] * n_row
        + [jax.ShapeDtypeStruct((rows, 1), F32)] * 2,
        compiler_params=pltpu.CompilerParams(vmem_limit_bytes=NORM_VMEM),
        cost_estimate=pl.CostEstimate(
            flops=10 * work, bytes_accessed=4 * work, transcendentals=rows
        ),
        name="norm_block",
    )(row.reshape(1), x, gain_cols)


def shards(
    features, output_gradient, value_weight, gate_weight, mixer_weight, conv_kernel, layer_norm_gain
):
    utts, frames, width = features.shape
    model = layer_norm_gain.shape[0]
    n_row, n_col, n_dp = lax.axis_size("row"), lax.axis_size("col"), lax.axis_size("dp")
    row, col = lax.axis_index("row"), lax.axis_index("col")
    per_row = n_col // n_row
    depth = per_row * width
    narrow = width // n_row
    tokens = utts * frames
    shifts = range(1, n_row)

    def to_row(x, s):
        return lax.ppermute(x, "row", ring(n_row, s))

    def rolled(blocks, s):
        return [blocks[(k - s) % n_row] for k in range(n_row)]

    def placed(pieces):
        buffer = jnp.zeros((n_row,) + pieces[0].shape, pieces[0].dtype)
        for k, piece in enumerate(pieces):
            buffer = lax.dynamic_update_index_in_dim(buffer, piece, (row - k) % n_row, 0)
        return buffer.reshape((-1,) + pieces[0].shape[1:])

    own = features.reshape(tokens, width)
    own_grad = output_gradient.reshape(tokens, width)
    part = tokens // PARTS
    gathered = [
        lax.all_gather(own[i * part : (i + 1) * part], "col", axis=0) for i in range(PARTS)
    ]

    mixer_rows = mixer_weight.reshape(per_row, n_row, narrow, width)
    mixer_of = [
        lax.dynamic_index_in_dim(mixer_rows, (row - k) % n_row, 1, keepdims=False).reshape(
            per_row * narrow, width
        )
        for k in range(n_row)
    ]

    def by_narrow(x):
        return jnp.stack([x[:, p * narrow : (p + 1) * narrow] for p in range(per_row)])

    def mixed_part(rows, s):
        return by_narrow(dot_last(rows, mixer_of[-s % n_row]).astype(BF16))

    grads = [own_grad] + [to_row(own_grad, s) for s in shifts]
    grad_rows = jnp.concatenate(grads)
    mixed_parts = [jnp.concatenate([mixed_part(g, 0) for g in grads], 1)]
    for s in shifts:
        sent = [mixed_part(g, s) for g in grads]
        arrived = [to_row(sent[(k - s) % n_row], s) for k in range(n_row)]
        mixed_parts.append(jnp.concatenate(arrived, 1))
    mixed_parts = jnp.concatenate(by_source(mixed_parts, "row"))

    gain_cols = layer_norm_gain.reshape(n_col, 1, width)
    means, inverses, kept, crossed, sent_out = [], [], [], [], []
    for x in gathered:
        if crossed:
            x = after(x, *crossed[-1])
        *pieces, mean, inverse = norm_block(row, x, gain_cols, n_row)
        kept.append(pieces[0])
        sent_out.append(pieces[1:])
        crossed.append([to_row(x, s) for s, x in zip(shifts, pieces[1:])])
        means.append(mean)
        inverses.append(inverse)
    mean, inverse = jnp.concatenate(means), jnp.concatenate(inverses)
    normed_own = jnp.concatenate(kept)
    normed_in = [jnp.concatenate([c[s - 1] for c in crossed]) for s in shifts]
    normed = jnp.concatenate([normed_own] + normed_in)

    mixed_grad = lax.psum_scatter(
        mixed_parts.reshape(n_col * n_row * tokens, narrow),
        "col",
        scatter_dimension=0,
        tiled=True,
    )

    count = HALVES if narrow % (HALVES * 128) == 0 else 1
    piece = narrow // count
    gate_own, value_own = dot(normed_own, gate_weight), dot(normed_own, value_weight)
    rest = jnp.concatenate(normed_in)
    gate_rest, value_rest = dot(rest, gate_weight), dot(rest, value_weight)

    def blocks_of(first, others):
        return [first] + [others[k * tokens : (k + 1) * tokens] for k in range(n_row - 1)]

    def reduced(blocks, q, dtype, *others):
        total = None
        for s in shifts:
            start = ((row + s) % n_row) * narrow + q * piece
            sent = [
                after(lax.dynamic_slice_in_dim(x, start, piece, 1).astype(dtype), *others)
                for x in blocks
            ]
            arrived = [to_row(sent[(k - s) % n_row], s) for k in range(n_row)]
            if total is None:
                total = arrived
            else:
                total = [t.astype(F32) + x.astype(F32) for t, x in zip(total, arrived)]
        return total

    gate, value = blocks_of(gate_own, gate_rest), blocks_of(value_own, value_rest)
    gate_in, value_in = [], []
    for q in range(count):
        before = gate_in[-1] + value_in[-1] if q else []
        gate_in.append(reduced(gate, q, F32, *before))
        value_in.append(reduced(value, q, BF16, *before))

    share = depth // n_dp

    def spread(x):
        return jnp.concatenate(
            exchange(lambda j: lax.dynamic_slice_in_dim(x, j * share, share, 1), "dp")
        )

    def collect(x):
        return jnp.concatenate(exchange(lambda j: x, "dp"))

    normed_cells, grad_cells = spread(normed), collect(grad_rows)
    mixed_grad = after(mixed_grad, normed_cells, grad_cells)
    done = []
    for q in range(count):
        here = [[after(x, *done) for x in y[q]] for y in (value_in, gate_in)]
        done = conv_block(
            row, value, here[0], gate, here[1], mixed_grad, conv_kernel, frames, count, q, done
        )
    mixed, pair, kernel_rows = done

    pair_blocks = [pair[k] for k in range(n_row)]
    first_in, second_in = [], []
    for s in shifts:
        order = rolled(pair_blocks, s)
        first_in.append([to_row(x, s) for x in order[1:]])
    for s in shifts:
        order = rolled(pair_blocks, s)
        second_in.append(to_row(after(order[0], *[x for y in first_in for x in y]), s))
    mixed_all = lax.all_gather(mixed, "col", axis=0)

    pair_kept = [after(x, *[y for z in first_in for y in z]) for x in pair_blocks]

    def wide(i, k):
        pieces = [pair_kept[k]] + [
            second_in[s - 1] if k == 0 else first_in[s - 1][k - 1] for s in shifts
        ]
        return jnp.concatenate(by_source([x[i] for x in pieces], "row"), axis=1)

    value_others = jnp.concatenate([wide(0, k) for k in range(1, n_row)])
    gate_others = jnp.concatenate([wide(1, k) for k in range(1, n_row)])
    part_others = back_block(value_others, gate_others, value_weight, gate_weight)
    part_in = []
    for s in shifts:
        k = n_row - 1 - s
        part_in.append(to_row(part_others[:, k * tokens : (k + 1) * tokens], s))
    second_in = [after(x, part_others) for x in second_in]
    value_mine, gate_mine = wide(0, 0), wide(1, 0)
    part_mine = back_block(value_mine, gate_mine, value_weight, gate_weight)
    def weight_grad(left, right):
        return lax.dot_general(left, right, CONTRACT_FIRST, preferred_element_type=F32)

    value_weight_grad = weight_grad(
        normed_cells, collect(jnp.concatenate([value_mine, value_others]))
    )

    mixed_all = after(mixed_all, value_weight_grad)

    def mixed_piece(j, k):
        return lax.dynamic_slice(
            mixed_all, (j * per_row, k * tokens, 0), (per_row, tokens, narrow)
        )

    mixed_out = [
        jnp.concatenate(
            [mixed_piece((row + s) % n_row, (k - s) % n_row) for k in range(n_row)], axis=1
        )
        for s in shifts
    ]
    part_in = [after(x, *mixed_out) for x in part_in]
    parts = placed([part_mine] + part_in)
    summed = lax.psum_scatter(
        parts.reshape(n_col * tokens, width), "col", scatter_dimension=0, tiled=True
    )

    mixed_in = [to_row(after(x, *part_in), s) for s, x in zip(shifts, mixed_out)]

    def side_by_side(x):
        return jnp.concatenate([x[p] for p in range(per_row)], axis=1)

    mixed_kept = side_by_side(lax.dynamic_slice_in_dim(mixed_all, row * per_row, per_row, 0))
    projected = dot(mixed_kept, mixer_of[0])

    gate_weight_grad = weight_grad(
        after(normed_cells, *part_in), collect(jnp.concatenate([gate_mine, gate_others]))
    )
    parts_wide = after(parts, gate_weight_grad).astype(F32)
    standard = (jnp.concatenate(gathered, axis=1).astype(F32) - mean) * inverse
    along = parts_wide * standard
    sums = jnp.stack([jnp.sum(parts_wide * gain_cols, (0, 2)), jnp.sum(along * gain_cols, (0, 2))])
    gain_sum = jnp.sum(along, 1)
    mixed_blocks = [mixed_kept]
    for s, piece in zip(shifts, mixed_in):
        mixed_blocks.append(side_by_side(after(piece, gate_weight_grad, projected)))
        projected = projected + dot(mixed_blocks[-1], mixer_of[s])
    small = exchange(
        lambda j: jnp.concatenate(
            [sums.reshape(-1), lax.dynamic_index_in_dim(gain_sum, j, 0, keepdims=False)]
        ),
        "col",
    )
    small = sum(small[1:], small[0])
    sums, gain_col = small[: 2 * tokens].reshape(2, tokens), small[2 * tokens :]
    gain_col = sum_over(gain_col, "dp")
    gain_pieces = exchange(lambda j: gain_col, "row")
    gain_pieces = [gain_pieces[0]] + [after(x, projected) for x in gain_pieces[1:]]
    norm_gain_gradient = sum(gain_pieces[1:], gain_pieces[0])
    projected_blocks = [projected[k * tokens : (k + 1) * tokens] for k in range(n_row)]
    total = own.astype(F32) + projected_blocks[0]
    for s in shifts:
        total = total + to_row(projected_blocks[-s % n_row].astype(BF16), s).astype(F32)
    module_out = total.astype(BF16).reshape(features.shape)

    mixed_sources = by_source(mixed_blocks, "row")
    mixed_rows = jnp.concatenate(
        [
            mixed_sources[h][:, p * narrow : (p + 1) * narrow]
            for p in range(per_row)
            for h in range(n_row)
        ],
        axis=1,
    )
    mixer_weight_grad = weight_grad(spread(mixed_rows), grad_cells)

    kernel_sum = sum_over(after(kernel_rows, *part_in), "dp")
    kernel_pieces = exchange(lambda j: kernel_sum, "row")
    kernel_pieces = [kernel_pieces[0]] + [after(x, projected) for x in kernel_pieces[1:]]
    kernel_grad = jnp.concatenate(by_source(kernel_pieces, "row"), axis=1)

    normed_grad = summed.astype(F32)
    own_standard = (own.astype(F32) - mean) * inverse
    gain_own = lax.dynamic_slice_in_dim(layer_norm_gain, col * width, width, 0)
    scaled = normed_grad * gain_own
    input_gradient = (
        own_grad.astype(F32)
        + (scaled - sums[0][:, None] / model - own_standard * (sums[1][:, None] / model)) * inverse
    )
    input_gradient = input_gradient.astype(BF16).reshape(features.shape)
    return (
        module_out,
        input_gradient,
        value_weight_grad,
        gate_weight_grad,
        mixer_weight_grad,
        kernel_grad,
        norm_gain_gradient,
    )


def solution(mesh):
    placed = (
        P(("groups", "dp"), "row", "col"),
        P(("groups", "dp"), "row", "col"),
        P("row", "col"),
        P("row", "col"),
        P("row", "col"),
        P(None, "col"),
        P(),
    )
    return jax.shard_map(
        shards,
        mesh=mesh,
        in_specs=placed,
        out_specs=(
            P(("groups", "dp"), "row", "col"),
            P(("groups", "dp"), "row", "col"),
            P(("groups", "row", "dp"), "col"),
            P(("groups", "row", "dp"), "col"),
            P(("groups", "row", "dp"), "col"),
            P("groups", "col"),
            P(("groups", "col")),
        ),
        check_vma=False,
    )
```
